32 devices in a mesh: dz: 4 (over x, core), dxy: 8 (over z, y).
Axes of the slice: x: 2, y: 2, z: 4, core: 2. Of those that a mesh axis runs over, the one named last changes fastest.
Arguments:
- queries: bfloat16 [4096, 1024], P(('dz', 'dxy')), may hold values from -180 to 180
- keys: bfloat16 [4096, 1024], P(('dz', 'dxy')), may hold values from -4 to 4
- values: bfloat16 [4096, 1024], P(('dz', 'dxy')), may hold values from -6 to 6
- out_grad: bfloat16 [4096, 1024], P(('dz', 'dxy')), may hold values from -6 to 6
- out_weight: bfloat16 [1024, 1024], replicated, may hold values from -0.1875 to 0.1875
- pair_counts: int32 [32, 9], P(('dz', 'dxy')), may hold values from 0 to 128, as said below
- counts: int32 [32], P(('dz', 'dxy')), may hold values from 2 to 128
Outputs:
- gradient_of_queries: bfloat16 [4096, 1024], P(('dz', 'dxy'))
- gradient_of_keys: bfloat16 [4096, 1024], P(('dz', 'dxy'))
- gradient_of_values: bfloat16 [4096, 1024], P(('dz', 'dxy'))
- wo_grad: float32 [1024, 1024], P('dxy')
The draws below stay inside these ranges and needn't reach their ends.
Inputs may be any that keep to these rules, and one draw needn't show every extreme that they name: `pair_counts`: slot ((i + 1) * 3 + (j + 1)) + t of cell c refers to cell t of the domain at offset (i, j) from c's domain; its entry is that cell's entry of counts when the two cells are linked, else 0, and always 0 where the domain lies outside the grid. Links are symmetric and every cell is linked to itself.
All inputs are finite; a program needn't handle non-finite values.
Results may differ from the reference program's by a relative error of at most 0.02.
Values may be sent and summed in bfloat16 or wider, within the bound.
No kernel may reach another device: no remote copies, remote signals or barrier semaphores. Data moves between devices by JAX's collectives and lax.ppermute only.
A program may use at most 128 MiB of HBM per device.

```python
import jax
import jax.numpy as jnp
from jax import lax

D = 1024
HEADS = 16
HEAD_DIM = 64
CELL = 128
CPD = 1
NB = 9
CELLS = 32
ATOMS = 4096
N_DZ = 4
N_DXY = 8


def cell_tables(key):
    base_key = jax.random.fold_in(key, 11)
    key_raw, key_pore, key_link = jax.random.split(base_key, 3)
    cell_total = CPD * N_DZ * N_DXY
    cell_ids = jnp.arange(cell_total, dtype=jnp.int32)
    raw_fill = jax.random.randint(key_raw, (cell_total,), 0, CELL - 1)
    layer_index = cell_ids // CPD // N_DXY
    factor = jnp.where(layer_index == N_DZ - 1, 1, 8)
    pore_mask = jax.random.randint(key_pore, (cell_total,), 0, 8) == 0
    factor = jnp.where(pore_mask, 1, factor)
    filled = 2 + raw_fill * factor // 8
    filled = filled.at[0].set(CELL).astype(jnp.int32)
    colour = jax.random.randint(key_link, (cell_total,), 0, 3)
    slot_ids = jnp.arange(9 * CPD, dtype=jnp.int32)
    offset_z = slot_ids // (3 * CPD) - 1
    offset_xy = slot_ids // CPD % 3 - 1
    local_cell = slot_ids % CPD
    domain = cell_ids // CPD
    layer_z = domain[:, None] // N_DXY + offset_z[None, :]
    place_xy = domain[:, None] % N_DXY + offset_xy[None, :]
    inside = (layer_z >= 0) & (layer_z < N_DZ) & (place_xy >= 0) & (place_xy < N_DXY)
    neighbour = (jnp.clip(layer_z, 0, N_DZ - 1) * N_DXY + jnp.clip(place_xy, 0, N_DXY - 1)) * CPD + local_cell[None, :]
    linked = (neighbour == cell_ids[:, None]) | ((colour[:, None] + colour[neighbour]) % 3 != 0)
    pair_table = jnp.where(inside & linked, filled[neighbour], 0).astype(jnp.int32)
    return (filled, pair_table)


def draw_counts(key, part):
    return cell_tables(key)[0]


def draw_pair_counts(key, part):
    return cell_tables(key)[1]


def query_key_pair(key):
    base_key = jax.random.fold_in(key, 23)
    key_first, key_second = jax.random.split(base_key)
    atom_total = CELL * CPD * N_DZ * N_DXY
    key_rows = jnp.clip(jax.random.normal(key_first, (atom_total, D), jnp.float32), -4.0, 4.0)
    query_rows = 2.0 * jnp.clip(jax.random.normal(key_second, (atom_total, D), jnp.float32), -4.0, 4.0)
    return (query_rows, key_rows)


def draw_queries(key, part):
    return query_key_pair(key)[0].astype(jnp.bfloat16)


def draw_keys(key, part):
    return query_key_pair(key)[1].astype(jnp.bfloat16)


def strengthened(values, stream_key, source, target, blocks, factor):
    owner, partner = [(jnp.arange(values.shape[axis_at]) // (values.shape[axis_at] // blocks)).reshape([-1 if axis == axis_at else 1 for axis in range(values.ndim)]) for axis_at in (source, target)]
    chosen = jax.random.permutation(stream_key, blocks)[partner]
    strong = (owner == chosen) | (owner == (partner + blocks // 2) % blocks)
    return jnp.where(strong, factor * values, values)


def level_of(stream_key, shape, shards, low, largest):
    factor_of = 1.0
    for dim, shards_of in shards:
        steps = jax.random.uniform(jax.random.fold_in(jax.random.fold_in(stream_key, 6), dim), (shards_of,), jnp.float32, low / len(shards), largest / len(shards))
        factor_of = factor_of * jnp.repeat(jnp.exp(steps), shape[dim] // shards_of).reshape((-1,) + (1,) * (len(shape) - 1 - dim))
    return factor_of


def normal_values(stream_key, shape, scale, most, pieces=(), held_as=jnp.bfloat16):
    loudness = level_of(stream_key, shape, pieces, -0.22, 0.18) if pieces else 1.0
    array = jax.random.normal(stream_key, shape, jnp.float32) * scale * loudness
    return jnp.minimum(jnp.maximum(array, -most), most).astype(held_as)


def bell_draw_with(key, extent, scale, most, cuts, heavy, kind=jnp.bfloat16):
    array = scale * jax.random.normal(key, extent, jnp.float32)
    if cuts:
        array = array * level_of(key, extent, cuts, -0.22, 0.18)
    return jnp.clip(strengthened(array, jax.random.fold_in(key, 3), *heavy), -most, most).astype(kind)


def setup_inputs(seed: int = 0) -> dict:
    key_of = jax.random.split(jax.random.key(seed), 8)
    return {
        "queries": draw_queries(jax.random.fold_in(key_of[7], 71), 0),
        "keys": draw_keys(jax.random.fold_in(key_of[7], 71), 0),
        "values": normal_values(key_of[2], (ATOMS, D), 1.0, 6.0, ((0, 32),)),
        "out_grad": bell_draw_with(key_of[3], (ATOMS, D), 1.0, 6.0, ((0, 32),), (0, 1, 32, 2.75)),
        "out_weight": normal_values(key_of[4], (D, D), D ** -0.5, 0.1875),
        "pair_counts": draw_pair_counts(jax.random.fold_in(key_of[7], 71), 0),
        "counts": draw_counts(jax.random.fold_in(key_of[7], 71), 0),
    }


def neighbour_cells(cell_ids):
    slot_ids = jnp.arange(NB, dtype=jnp.int32)
    offset_z = slot_ids // (3 * CPD) - 1
    offset_xy = (slot_ids // CPD) % 3 - 1
    local_cell = slot_ids % CPD
    domain = cell_ids // CPD
    layer_z = domain[:, None] // N_DXY + offset_z[None, :]
    place_xy = domain[:, None] % N_DXY + offset_xy[None, :]
    inside = (layer_z >= 0) & (layer_z < N_DZ) & (place_xy >= 0) & (place_xy < N_DXY)
    target = (jnp.clip(layer_z, 0, N_DZ - 1) * N_DXY + jnp.clip(place_xy, 0, N_DXY - 1)) * CPD + local_cell[None, :]
    return target.astype(jnp.int32), inside


def reference(queries, keys, values, out_grad, out_weight, pair_counts, counts):
    logit_scale = HEAD_DIM ** -0.5
    atom_index = jnp.arange(CELL, dtype=jnp.int32)
    live_rows = (atom_index[None, :] < counts[:, None]).reshape(ATOMS, 1)
    masked_grad = jnp.where(live_rows, out_grad, jnp.zeros_like(out_grad))
    out_delta = jnp.dot(masked_grad, out_weight, preferred_element_type=jnp.float32).astype(jnp.bfloat16)
    cell_shape = (CELLS, CELL, HEADS, HEAD_DIM)
    query_cells = queries.reshape(cell_shape)
    key_cells = keys.reshape(cell_shape)
    value_cells = values.reshape(cell_shape)
    delta_cells = out_delta.reshape(cell_shape)
    cell_ids = jnp.arange(CELLS, dtype=jnp.int32)
    target, inside = neighbour_cells(cell_ids)

    def query_side(cell_id):
        near_cells = target[cell_id]
        adjacent_keys = key_cells[near_cells].reshape(NB * CELL, HEADS, HEAD_DIM).astype(jnp.float32)
        adjacent_values = value_cells[near_cells].reshape(NB * CELL, HEADS, HEAD_DIM).astype(jnp.float32)
        allowed = (atom_index[None, :] < pair_counts[cell_id][:, None]).reshape(NB * CELL)
        home_cell_queries = query_cells[cell_id].astype(jnp.float32)
        home_cell_delta = delta_cells[cell_id].astype(jnp.float32)
        attention_logits = logit_scale * jnp.einsum("qvy,pvy->vqp", home_cell_queries, adjacent_keys)
        attention_logits = jnp.where(allowed[None, None, :], attention_logits, -1e30)
        highest = jnp.max(attention_logits, axis=-1, keepdims=True)
        weight_sum = jnp.sum(jnp.where(allowed[None, None, :], jnp.exp(attention_logits - highest), 0.0), axis=-1, keepdims=True)
        log_total = highest + jnp.log(weight_sum)
        probs = jnp.where(allowed[None, None, :], jnp.exp(attention_logits - log_total), 0.0)
        probabilities_reduced = probs.astype(jnp.bfloat16)
        attention_result = jnp.einsum("gtl,lgs->tgs", probabilities_reduced.astype(jnp.float32), adjacent_values).astype(jnp.bfloat16)
        row_delta = jnp.sum(home_cell_delta * attention_result.astype(jnp.float32), axis=-1)
        probability_gradient = jnp.einsum("qvy,pvy->vqp", home_cell_delta, adjacent_values)
        score_gradient = (probs * (probability_gradient - row_delta.T[:, :, None])).astype(jnp.bfloat16)
        gradient_of_queries = (logit_scale * jnp.einsum("gtl,lgs->tgs", score_gradient.astype(jnp.float32), adjacent_keys)).astype(jnp.bfloat16)
        return gradient_of_queries.reshape(CELL, D), attention_result.reshape(CELL, D), log_total[:, :, 0], row_delta.T

    query_grads, attended_cells, log_totals, row_deltas = lax.map(query_side, cell_ids)

    def key_side(cell_id):
        near_cells = target[cell_id]
        near_inside = inside[cell_id]
        reverse_slot = ((8 - jnp.arange(NB, dtype=jnp.int32) // CPD) * CPD + cell_id % CPD).astype(jnp.int32)
        limit = jnp.where(near_inside, pair_counts[near_cells, reverse_slot], 0)
        allowed = jnp.broadcast_to(atom_index[None, None, :] < limit[:, None, None], (NB, CELL, CELL)).reshape(NB * CELL, CELL)
        adjacent_queries = query_cells[near_cells].reshape(NB * CELL, HEADS, HEAD_DIM).astype(jnp.float32)
        adjacent_delta = delta_cells[near_cells].reshape(NB * CELL, HEADS, HEAD_DIM).astype(jnp.float32)
        near_lse = jnp.transpose(log_totals[near_cells], (1, 0, 2)).reshape(HEADS, NB * CELL)
        near_rows = jnp.transpose(row_deltas[near_cells], (1, 0, 2)).reshape(HEADS, NB * CELL)
        home_cell_keys = key_cells[cell_id].astype(jnp.float32)
        home_cell_values = value_cells[cell_id].astype(jnp.float32)
        attention_logits = logit_scale * jnp.einsum("sfc,nfc->fsn", adjacent_queries, home_cell_keys)
        probs = jnp.where(allowed[None], jnp.exp(jnp.where(allowed[None], attention_logits - near_lse[:, :, None], 0.0)), 0.0)
        probabilities_reduced = probs.astype(jnp.bfloat16)
        probability_gradient = jnp.einsum("sfc,nfc->fsn", adjacent_delta, home_cell_values)
        score_gradient = (probs * (probability_gradient - near_rows[:, :, None])).astype(jnp.bfloat16)
        gradient_of_values = jnp.einsum("ucy,cuo->yuo", probabilities_reduced.astype(jnp.float32), adjacent_delta)
        gradient_of_keys = logit_scale * jnp.einsum("ucy,cuo->yuo", score_gradient.astype(jnp.float32), adjacent_queries)
        return gradient_of_keys.reshape(CELL, D).astype(jnp.bfloat16), gradient_of_values.reshape(CELL, D).astype(jnp.bfloat16)

    key_grads, value_grads = lax.map(key_side, cell_ids)
    attended_all = attended_cells.reshape(ATOMS, D)
    wo_grad = lax.dot_general(masked_grad, attended_all, (((0,), (0,)), ((), ())), preferred_element_type=jnp.float32) * ATOMS ** -0.5
    return query_grads.reshape(ATOMS, D), key_grads.reshape(ATOMS, D), value_grads.reshape(ATOMS, D), wo_grad
```

```python
import jax
import jax.numpy as jnp
from jax import lax
from jax.experimental import pallas as pl
from jax.experimental.pallas import tpu as pltpu
from jax.sharding import PartitionSpec as P

HEADS = 16
CELL = 128
PAIR = 2
NEAR = 9


NT = (((1,), (1,)), ((), ()))
NN = (((1,), (0,)), ((), ()))


def even_pairs(count):
    pairs = [(i, i + 1) for i in range(0, count - 1, 2)]
    return pairs + [(b, a) for a, b in pairs]


def odd_pairs(count):
    pairs = [(i, i + 1) for i in range(1, count - 1, 2)]
    return pairs + [(b, a) for a, b in pairs]


def far_pairs(count, by):
    return [(i, i ^ by) for i in range(count) if (i ^ by) < count]


def relay_pairs(count):
    pairs = [(i, i + 2) for i in range(0, count - 2, 2)]
    return pairs + [(i, i - 2) for i in range(3, count, 2)]


def stacked_heads(block, lane):
    zero = jnp.zeros_like(block)
    half = block.shape[1] // PAIR
    return jnp.concatenate(
        [jnp.where(lane < half, block, zero), jnp.where(lane >= half, block, zero)], axis=0
    )


def query_side_kernel(limits, q_ref, do_ref, *refs):
    kv = refs[:NEAR]
    dq_ref, att_ref, rows_ref, cols_ref, s_ref = refs[NEAR:]
    step = pl.program_id(0)
    rows, width = q_ref.shape
    half = width // PAIR
    scale = half ** -0.5
    lane = lax.broadcasted_iota(jnp.int32, (rows, width), 1)
    wide_lane = lax.broadcasted_iota(jnp.int32, (PAIR * rows, CELL), 1)
    qs = stacked_heads((q_ref[...].astype(jnp.float32) * scale).astype(jnp.bfloat16), lane)
    do = do_ref[...]
    dos = stacked_heads(do, lane)
    high = jnp.full((PAIR * rows, CELL), -1e30, jnp.float32)
    for k in range(NEAR):
        s = lax.dot_general(qs, kv[k][0], NT, preferred_element_type=jnp.float32)
        s = jnp.where(wide_lane < limits[k], s, -1e30)
        s_ref[k] = s
        high = jnp.maximum(high, s)
    top = jnp.max(high, axis=1, keepdims=True)
    total = jnp.zeros((PAIR * rows, CELL), jnp.float32)
    out = jnp.zeros((PAIR * rows, width), jnp.float32)
    for k in range(NEAR):
        p = jnp.exp(s_ref[k] - top)
        s_ref[k] = p
        total = total + p
        out = out + lax.dot_general(
            p.astype(jnp.bfloat16), kv[k][1], NN, preferred_element_type=jnp.float32
        )
    weight = jnp.sum(total, axis=1, keepdims=True)
    inverse = 1.0 / weight
    out = out * inverse
    att = jnp.where(lane < half, out[:rows], out[rows:]).astype(jnp.bfloat16)
    att_ref[...] = att
    product = do.astype(jnp.float32) * att.astype(jnp.float32)
    low = jnp.sum(jnp.where(lane < half, product, 0.0), axis=1, keepdims=True)
    upper = jnp.sum(jnp.where(lane >= half, product, 0.0), axis=1, keepdims=True)
    delta = jnp.concatenate([low, upper], axis=0)
    lse = top + jnp.log(weight)
    grad = jnp.zeros((PAIR * rows, width), jnp.float32)
    for k in range(NEAR):
        dp = lax.dot_general(dos, kv[k][1], NT, preferred_element_type=jnp.float32)
        ds = (s_ref[k] * ((dp - delta) * inverse)).astype(jnp.bfloat16)
        grad = grad + lax.dot_general(ds, kv[k][0], NN, preferred_element_type=jnp.float32)
    dq = jnp.where(lane < half, grad[:rows], grad[rows:]) * scale
    dq_ref[...] = dq.astype(jnp.bfloat16)
    base = step * (2 * PAIR)
    cols = jnp.where(step == 0, jnp.zeros_like(cols_ref), cols_ref[...])
    for t, value in enumerate((lse[:rows], lse[rows:], low, upper)):
        cols = jnp.where(lane == base + t, value, cols)
    cols_ref[...] = cols

    @pl.when(step == pl.num_programs(0) - 1)
    def _():
        rows_ref[...] = cols.T[: rows_ref.shape[0]]


def key_side_kernel(limits, kv_ref, *refs):
    qdo = refs[:NEAR]
    stats = refs[NEAR : 2 * NEAR]
    dk_ref, dv_ref = refs[2 * NEAR :]
    step = pl.program_id(0)
    rows, width = dk_ref.shape
    half = width // PAIR
    scale = half ** -0.5
    base = step * (2 * PAIR)
    lane = lax.broadcasted_iota(jnp.int32, (rows, width), 1)
    row = lax.broadcasted_iota(jnp.int32, (rows, PAIR * CELL), 0)
    own_keys = kv_ref[0]
    own_values = kv_ref[1]
    dk = jnp.zeros((rows, width), jnp.float32)
    dv = jnp.zeros((rows, width), jnp.float32)
    for k in range(NEAR):
        qs = stacked_heads((qdo[k][0].astype(jnp.float32) * scale).astype(jnp.bfloat16), lane)
        dos = stacked_heads(qdo[k][1], lane)
        lse = jnp.concatenate(
            [stats[k][pl.ds(base, 1), :], stats[k][pl.ds(base + 1, 1), :]], axis=1
        )
        delta = jnp.concatenate(
            [stats[k][pl.ds(base + 2, 1), :], stats[k][pl.ds(base + 3, 1), :]], axis=1
        )
        s = lax.dot_general(own_keys, qs, NT, preferred_element_type=jnp.float32)
        p = jnp.where(row < limits[k], jnp.exp(s - lse), 0.0)
        dp = lax.dot_general(own_values, dos, NT, preferred_element_type=jnp.float32)
        ds = (p * (dp - delta)).astype(jnp.bfloat16)
        dv = dv + lax.dot_general(
            p.astype(jnp.bfloat16), dos, NN, preferred_element_type=jnp.float32
        )
        dk = dk + lax.dot_general(ds, qs, NN, preferred_element_type=jnp.float32)
    dk_ref[...] = dk.astype(jnp.bfloat16)
    dv_ref[...] = dv.astype(jnp.bfloat16)


def query_side(limits, q, do, kv):
    rows, model_width = q.shape
    pairs = HEADS // PAIR
    width = model_width // pairs
    stat_rows = pairs * 2 * PAIR
    column = pl.BlockSpec((rows, width), lambda i, lim: (0, i))
    double = pl.BlockSpec((2, CELL, width), lambda i, lim: (0, 0, i))
    flat = jax.ShapeDtypeStruct((rows, model_width), jnp.bfloat16)
    dq, att, stats, _ = pl.pallas_call(
        query_side_kernel,
        grid_spec=pltpu.PrefetchScalarGridSpec(
            num_scalar_prefetch=1,
            grid=(pairs,),
            in_specs=[column, column] + [double] * NEAR,
            out_specs=[
                column,
                column,
                pl.BlockSpec((stat_rows, rows), lambda i, lim: (0, 0)),
                pl.BlockSpec((rows, CELL), lambda i, lim: (0, 0)),
            ],
            scratch_shapes=[
                pltpu.VMEM((NEAR, PAIR * rows, CELL), jnp.float32),
            ],
        ),
        out_shape=[
            flat,
            flat,
            jax.ShapeDtypeStruct((stat_rows, rows), jnp.float32),
            jax.ShapeDtypeStruct((rows, CELL), jnp.float32),
        ],
        cost_estimate=pl.CostEstimate(
            flops=8 * NEAR * rows * CELL * model_width,
            bytes_accessed=(4 + 2 * NEAR) * rows * model_width * 2,
            transcendentals=NEAR * rows * CELL * HEADS,
        ),
        name="query_side",
    )(limits, q, do, *kv)
    return dq, att, stats


def key_side(limits, own_kv, qdo, stats):
    _, rows, model_width = own_kv.shape
    pairs = HEADS // PAIR
    width = model_width // pairs
    column = pl.BlockSpec((rows, width), lambda i, lim: (0, i))
    double = pl.BlockSpec((2, CELL, width), lambda i, lim: (0, 0, i))
    whole = pl.BlockSpec(stats[0].shape, lambda i, lim: (0, 0))
    flat = jax.ShapeDtypeStruct((rows, model_width), jnp.bfloat16)
    return pl.pallas_call(
        key_side_kernel,
        grid_spec=pltpu.PrefetchScalarGridSpec(
            num_scalar_prefetch=1,
            grid=(pairs,),
            in_specs=[double] + [double] * NEAR + [whole] * NEAR,
            out_specs=[column, column],
        ),
        out_shape=[flat, flat],
        cost_estimate=pl.CostEstimate(
            flops=8 * NEAR * rows * CELL * model_width,
            bytes_accessed=(4 + 2 * NEAR) * rows * model_width * 2,
            transcendentals=NEAR * rows * CELL * HEADS,
        ),
        name="key_side",
    )(limits, own_kv, *qdo, *stats)


def sent(value, axis, pairs):
    return lax.ppermute(value, axis, pairs)


def in_plane(value, relay):
    count = lax.axis_size("dxy")
    even = sent(value, "dxy", even_pairs(count))
    if relay:
        odd = sent(even, "dxy", relay_pairs(count))
    else:
        odd = sent(value, "dxy", odd_pairs(count))
    return [value, even, odd]


def around(value, relay):
    count = lax.axis_size("dz")
    columns = in_plane(value, relay)
    even = [sent(v, "dz", even_pairs(count)) for v in columns]
    odd = [sent(v, "dz", odd_pairs(count)) for v in columns]
    return columns + even + odd


def shards(queries, keys, values, out_grad, out_weight, pair_counts, counts):
    row_count, model_width = queries.shape
    layer = lax.axis_index("dz")
    place = lax.axis_index("dxy")
    atom_index = jnp.arange(CELL, dtype=jnp.int32)
    table = pair_counts.reshape(3, 3)
    table = jnp.where(
        layer % 2 == 0, table[jnp.array([1, 2, 0])], table[jnp.array([1, 0, 2])]
    )
    table = jnp.where(
        place % 2 == 0, table[:, jnp.array([1, 2, 0])], table[:, jnp.array([1, 0, 2])]
    )
    near_limits = table.reshape(NEAR)
    own_limits = jnp.where(near_limits > 0, counts[0], 0)
    live_rows = (atom_index[None, :] < counts[:, None]).reshape(row_count, 1)
    masked_grad = jnp.where(live_rows, out_grad, jnp.zeros_like(out_grad))
    out_delta = jnp.dot(masked_grad, out_weight, preferred_element_type=jnp.float32).astype(
        jnp.bfloat16
    )
    kv = around(jnp.stack([keys, values]), True)
    qdo = around(jnp.stack([queries, out_delta]), True)
    dq, att, stats = query_side(near_limits, queries, out_delta, kv)
    near_stats = around(stats, False)
    dk, dv = key_side(own_limits, kv[0], qdo, near_stats)
    device_count = lax.axis_size("dz") * lax.axis_size("dxy")
    normalizer = (row_count * device_count) ** (-0.5)
    plane_rows = lax.psum_scatter(
        lax.dot_general(
            masked_grad, att, (((0,), (0,)), ((), ())), preferred_element_type=jnp.float32
        ),
        "dxy",
        scatter_dimension=0,
        tiled=True,
    )
    wo_grad = lax.psum(plane_rows, "dz") * normalizer
    return dq, dk, dv, wo_grad


def solution(mesh):
    in_specs = (
        P(("dz", "dxy"), None),
        P(("dz", "dxy"), None),
        P(("dz", "dxy"), None),
        P(("dz", "dxy"), None),
        P(),
        P(("dz", "dxy"), None),
        P(("dz", "dxy")),
    )
    out_specs = (
        P(("dz", "dxy"), None),
        P(("dz", "dxy"), None),
        P(("dz", "dxy"), None),
        P("dxy", None),
    )
    return jax.shard_map(shards, mesh=mesh, in_specs=in_specs, out_specs=out_specs, check_vma=False)
```

```python
import jax
import jax.numpy as jnp
from jax import lax
from jax.experimental import pallas as pl
from jax.experimental.pallas import tpu as pltpu
from jax.sharding import PartitionSpec as P

HEADS = 16
CELL = 128
PAIR = 2
NEAR = 9


NT = (((1,), (1,)), ((), ()))
NN = (((1,), (0,)), ((), ()))


def dot(a,b,d): return lax.dot_general(a,b,d,preferred_element_type=jnp.float32)


def query_side_kernel(limits, q_ref, do_ref, *refs):
    k_refs, v_refs = refs[:NEAR], refs[NEAR:2*NEAR]
    dq_ref, att_ref, rows_ref, cols_ref, kcat, vcat = refs[2*NEAR:]
    step = pl.program_id(0)
    rows, width = q_ref.shape
    half = width // PAIR
    scale = half ** -0.5
    lane = lax.broadcasted_iota(jnp.int32, (rows, width), 1)
    for k in range(NEAR):
        kcat[pl.ds(k*CELL, CELL), :] = k_refs[k][...]
        vcat[pl.ds(k*CELL, CELL), :] = v_refs[k][...]
    slot = lax.broadcasted_iota(jnp.int32, (1, CELL), 1)
    bias = jnp.concatenate([jnp.where(slot < limits[k], 0.0, -1e30) for k in range(NEAR)], axis=1)
    q = q_ref[...]; q = (q.astype(jnp.float32) * scale).astype(jnp.bfloat16)
    do = do_ref[...]
    zero = jnp.zeros_like(q)
    outs, stats, parts = [], [], []
    for h in range(PAIR):
        mine = (lane < half) if h == 0 else (lane >= half)
        s = dot(jnp.where(mine, q, zero), kcat[...], NT) + bias
        top = jnp.max(s, axis=1, keepdims=True)
        p = jnp.exp(s - top)
        weight = jnp.sum(p, axis=1, keepdims=True)
        inverse = 1.0 / weight
        out = (dot(p.astype(jnp.bfloat16), vcat[...], NN) * inverse).astype(jnp.bfloat16)
        doh = jnp.where(mine, do, zero)
        delta = jnp.sum(doh.astype(jnp.float32) * out.astype(jnp.float32), axis=1, keepdims=True)
        dp = dot(doh, vcat[...], NT)
        ds = (p * (dp - delta)).astype(jnp.bfloat16)
        grad = dot(ds, kcat[...], NN) * (inverse * scale)
        outs.append(out); parts.append(grad); stats.append((top + jnp.log(weight), delta))
    att_ref[...] = jnp.where(lane < half, outs[0], outs[1])
    dq_ref[...] = jnp.where(lane < half, parts[0], parts[1]).astype(jnp.bfloat16)
    base = step * (2 * PAIR)
    cols = jnp.where(step == 0, jnp.zeros_like(cols_ref), cols_ref[...])
    for t, value in enumerate((stats[0][0], stats[1][0], stats[0][1], stats[1][1])):
        cols = jnp.where(lane == base + t, value, cols)
    cols_ref[...] = cols
    @pl.when(step == pl.num_programs(0) - 1)
    def _():
        rows_ref[...] = cols.T[: rows_ref.shape[0]]


def key_side_kernel(limits, k_ref, v_ref, *refs):
    q_refs, do_refs, stats = refs[:NEAR], refs[NEAR:2*NEAR], refs[2*NEAR:3*NEAR]
    dk_ref, dv_ref, qcat, docat = refs[3*NEAR:]
    step = pl.program_id(0)
    rows, width = dk_ref.shape
    half = width // PAIR
    scale = half ** -0.5
    base = step * (2 * PAIR)
    lane = lax.broadcasted_iota(jnp.int32, (rows, width), 1)
    live = lax.broadcasted_iota(jnp.int32, (rows, width), 0) < limits[NEAR]
    for k in range(NEAR):
        q = (q_refs[k][...].astype(jnp.float32) * scale).astype(jnp.bfloat16)
        do = do_refs[k][...]
        zero = jnp.zeros_like(q)
        for h in range(PAIR):
            mine = (lane < half) if h == 0 else (lane >= half)
            qcat[h, pl.ds(k*CELL, CELL), :] = jnp.where(mine, q, zero)
            docat[h, pl.ds(k*CELL, CELL), :] = jnp.where(mine, do, zero)
    own_keys = k_ref[...]; own_values = v_ref[...]
    dk = dv = None
    for h in range(PAIR):
        lse = jnp.concatenate([stats[k][pl.ds(base + h, 1), :] + jnp.where(limits[k] > 0, 0.0, 1e30) for k in range(NEAR)], axis=1)
        delta = jnp.concatenate([stats[k][pl.ds(base + PAIR + h, 1), :] for k in range(NEAR)], axis=1)
        s = dot(own_keys, qcat[h], NT)
        p = jnp.exp(s - lse)
        dp = dot(own_values, docat[h], NT)
        ds = (p * (dp - delta)).astype(jnp.bfloat16)
        a = dot(p.astype(jnp.bfloat16), docat[h], NN)
        b = dot(ds, qcat[h], NN)
        dv = a if dv is None else dv + a
        dk = b if dk is None else dk + b
    dk_ref[...] = jnp.where(live, dk, 0.0).astype(jnp.bfloat16)
    dv_ref[...] = jnp.where(live, dv, 0.0).astype(jnp.bfloat16)


def query_side(limits, q, do, ks, vs):
    rows, model_width = q.shape
    pairs = HEADS // PAIR
    width = model_width // pairs
    stat_rows = pairs * 2 * PAIR
    column = pl.BlockSpec((rows, width), lambda i, lim: (0, i))
    flat = jax.ShapeDtypeStruct((rows, model_width), jnp.bfloat16)
    dq, att, stats, _ = pl.pallas_call(
        query_side_kernel,
        grid_spec=pltpu.PrefetchScalarGridSpec(
            num_scalar_prefetch=1, grid=(pairs,),
            in_specs=[column] * (2 + 2*NEAR),
            out_specs=[column, column,
                pl.BlockSpec((stat_rows, rows), lambda i, lim: (0, 0)),
                pl.BlockSpec((rows, CELL), lambda i, lim: (0, 0))],
            scratch_shapes=[pltpu.VMEM((NEAR*CELL, width), jnp.bfloat16)]*2,
        ),
        out_shape=[flat, flat, jax.ShapeDtypeStruct((stat_rows, rows), jnp.float32), jax.ShapeDtypeStruct((rows, CELL), jnp.float32)],
        name="query_side",
    )(limits, q, do, *ks, *vs)
    return dq, att, stats


def key_side(limits, k, v, qs, dos, stats):
    rows, model_width = k.shape
    pairs = HEADS // PAIR
    width = model_width // pairs
    column = pl.BlockSpec((rows, width), lambda i, lim: (0, i))
    whole = pl.BlockSpec(stats[0].shape, lambda i, lim: (0, 0))
    flat = jax.ShapeDtypeStruct((rows, model_width), jnp.bfloat16)
    return pl.pallas_call(
        key_side_kernel,
        grid_spec=pltpu.PrefetchScalarGridSpec(
            num_scalar_prefetch=1, grid=(pairs,),
            in_specs=[column]*(2+2*NEAR) + [whole] * NEAR,
            out_specs=[column, column],
            scratch_shapes=[pltpu.VMEM((PAIR, NEAR*CELL, width), jnp.bfloat16)]*2,
        ),
        out_shape=[flat, flat],
        name="key_side",
    )(limits, k, v, *qs, *dos, *stats)


def even_pairs(count):
    pairs = [(i, i + 1) for i in range(0, count - 1, 2)]
    return pairs + [(b, a) for a, b in pairs]


def odd_pairs(count):
    pairs = [(i, i + 1) for i in range(1, count - 1, 2)]
    return pairs + [(b, a) for a, b in pairs]


def flip_pairs(count, bit):
    return [(i, i ^ bit) for i in range(count)]


def relay_pairs(count):
    pairs = [(i, i + 2) for i in range(0, count - 2, 2)]
    return pairs + [(i, i - 2) for i in range(3, count, 2)]


def stacked_layers(columns):
    count = lax.axis_size("dz")
    even = [lax.ppermute(v, "dz", even_pairs(count)) for v in columns]
    odd = [lax.ppermute(v, "dz", odd_pairs(count)) for v in columns]
    return columns + even + odd


def around(value, relay):
    count = lax.axis_size("dxy")
    even = lax.ppermute(value, "dxy", even_pairs(count))
    if relay:
        odd = lax.ppermute(even, "dxy", relay_pairs(count))
    else:
        odd = lax.ppermute(value, "dxy", odd_pairs(count))
    return stacked_layers([value, even, odd])


def in_partner_order(table, index, axis):
    low, own, high = (lax.index_in_dim(table, i, axis) for i in range(3))
    first = jnp.where(index % 2 == 0, high, low)
    second = jnp.where(index % 2 == 0, low, high)
    return jnp.concatenate([own, first, second], axis=axis)


def bit_reversed(count):
    bits = count.bit_length() - 1
    return [int(format(i, "b").zfill(bits)[::-1], 2) if bits else 0 for i in range(count)]


def weight_gradient(grad_rows, att, normalizer):
    layers = lax.axis_size("dz")
    places = lax.axis_size("dxy")
    layer = lax.axis_index("dz")
    place = lax.axis_index("dxy")
    atoms, width = att.shape
    slab = width // layers
    rows = width // places
    cells = [att]
    for bit in [1 << b for b in reversed(range(layers.bit_length() - 1))]:
        cells = cells + [lax.ppermute(c, "dz", flip_pairs(layers, bit)) for c in cells]
    mine = [lax.dynamic_slice_in_dim(c, layer * slab, slab, axis=1) for c in cells]
    part = lax.dot_general(
        grad_rows,
        jnp.concatenate(mine, axis=0),
        (((0,), (0,)), ((), ())),
        preferred_element_type=jnp.float32,
    ).reshape(places, rows, slab)
    bit = 1
    while bit < places:
        upper = (place // bit) % 2
        halves = part.reshape(2, part.shape[0] // 2, rows, slab)
        give = lax.dynamic_index_in_dim(halves, 1 - upper, 0, keepdims=False)
        keep = lax.dynamic_index_in_dim(halves, upper, 0, keepdims=False)
        got = lax.ppermute(give.astype(jnp.bfloat16), "dxy", flip_pairs(places, bit))
        part = keep.astype(jnp.float32) + got.astype(jnp.float32)
        bit *= 2
    own = (part * normalizer).reshape(rows, slab)
    held = [own]
    order = [0]
    for bit in [1 << b for b in reversed(range(layers.bit_length() - 1))]:
        held = held + [lax.ppermute(h, "dz", flip_pairs(layers, bit)) for h in held]
        order = order + [o ^ bit for o in order]
    result = []
    for target in range(layers):
        value = held[0]
        for h, o in zip(held[1:], order[1:]):
            value = jnp.where(layer == (target ^ o), h, value)
        result.append(value)
    return jnp.concatenate(result, axis=1)


def gathered_rows(masked_grad):
    layers = lax.axis_size("dz")
    places = lax.axis_size("dxy")
    atoms, width = masked_grad.shape
    cells = [masked_grad]
    for bit in [1 << b for b in reversed(range(layers.bit_length() - 1))]:
        cells = cells + [lax.ppermute(c, "dz", flip_pairs(layers, bit)) for c in cells]
    whole = jnp.concatenate(cells, axis=0).reshape(layers * atoms, places, width // places)
    whole = jnp.concatenate([whole[:, i : i + 1] for i in bit_reversed(places)], axis=1)
    return whole.reshape(layers * atoms, width)


def shards(queries, keys, values, out_grad, out_weight, pair_counts, counts):
    row_count, model_width = queries.shape
    layer = lax.axis_index("dz")
    place = lax.axis_index("dxy")
    atom_index = jnp.arange(CELL, dtype=jnp.int32)
    table = pair_counts.reshape(3, 3)
    near_limits = in_partner_order(in_partner_order(table, layer, 0), place, 1).reshape(NEAR)
    limits = jnp.concatenate([near_limits, counts])
    live_rows = (atom_index[None, :] < counts[:, None]).reshape(row_count, 1)
    masked_grad = jnp.where(live_rows, out_grad, jnp.zeros_like(out_grad))
    out_delta = jnp.dot(masked_grad, out_weight, preferred_element_type=jnp.float32).astype(
        jnp.bfloat16
    )
    near_keys = around(keys, True)
    near_values = around(values, True)
    near_queries = around(queries, True)
    near_delta = around(out_delta, True)
    grad_rows = gathered_rows(masked_grad)
    dq, att, stats = query_side(limits, queries, out_delta, near_keys, near_values)
    near_stats = around(stats, False)
    device_count = lax.axis_size("dz") * lax.axis_size("dxy")
    wo_grad = weight_gradient(grad_rows, att, (row_count * device_count) ** (-0.5))
    dk, dv = key_side(limits, keys, values, near_queries, near_delta, near_stats)
    return dq, dk, dv, wo_grad


def solution(mesh):
    in_specs = (
        P(("dz", "dxy"), None),
        P(("dz", "dxy"), None),
        P(("dz", "dxy"), None),
        P(("dz", "dxy"), None),
        P(),
        P(("dz", "dxy"), None),
        P(("dz", "dxy")),
    )
    out_specs = (
        P(("dz", "dxy"), None),
        P(("dz", "dxy"), None),
        P(("dz", "dxy"), None),
        P("dxy", None),
    )
    return jax.shard_map(shards, mesh=mesh, in_specs=in_specs, out_specs=out_specs, check_vma=False)
```

```python
import functools

import jax
import jax.numpy as jnp
from jax import lax
from jax.experimental import pallas as pl
from jax.experimental.pallas import tpu as pltpu
from jax.sharding import PartitionSpec as P

HEADS = 16
CELL = 128
PAIR = 2
NEAR = 9
CHUNKS = 2
KEY_PARTS = (3, 3, 2)


NT = (((1,), (1,)), ((), ()))
NN = (((1,), (0,)), ((), ()))
TN = (((0,), (0,)), ((), ()))


def dot(a, b, dims):
    return lax.dot_general(a, b, dims, preferred_element_type=jnp.float32)


def bits_of(count):
    return count.bit_length() - 1


def key_bias(limits):
    slot = lax.broadcasted_iota(jnp.int32, (1, CELL), 1)
    return jnp.concatenate(
        [jnp.where(slot < limits[k], 0.0, -1e30) for k in range(NEAR)], axis=1
    )


def load_near(refs, kcat, vcat):
    for k, (key_ref, value_ref) in enumerate(refs):
        kcat[pl.ds(k * CELL, CELL), :] = key_ref[...]
        vcat[pl.ds(k * CELL, CELL), :] = value_ref[...]


def query_side_kernel(limits, q_ref, do_ref, *refs):
    near = list(zip(refs[:NEAR], refs[NEAR : 2 * NEAR]))
    att_ref, dq_ref, rows_ref, cols_ref, kcat, vcat = refs[-6:]
    step = pl.program_id(0)
    rows, width = q_ref.shape
    half = width // PAIR
    scale = half**-0.5
    lane = lax.broadcasted_iota(jnp.int32, (rows, width), 1)
    load_near(near, kcat, vcat)
    bias = key_bias(limits)
    q = (q_ref[...].astype(jnp.float32) * scale).astype(jnp.bfloat16)
    do = do_ref[...]
    zero = jnp.zeros_like(q)
    outs, parts, lses, deltas = [], [], [], []
    for h in range(PAIR):
        mine = (lane < half) if h == 0 else (lane >= half)
        s = dot(jnp.where(mine, q, zero), kcat[...], NT) + bias
        top = jnp.max(s, axis=1, keepdims=True)
        p = jnp.exp(s - top)
        weight = jnp.sum(p, axis=1, keepdims=True)
        inverse = 1.0 / weight
        out = (dot(p.astype(jnp.bfloat16), vcat[...], NN) * inverse).astype(jnp.bfloat16)
        doh = jnp.where(mine, do, zero)
        delta = jnp.sum(doh.astype(jnp.float32) * out.astype(jnp.float32), axis=1, keepdims=True)
        dp = dot(doh, vcat[...], NT)
        ds = (p * (dp - delta)).astype(jnp.bfloat16)
        outs.append(out)
        parts.append(dot(ds, kcat[...], NN) * (inverse * scale))
        lses.append(top + jnp.log(weight))
        deltas.append(delta)
    att_ref[...] = jnp.where(lane < half, outs[0], outs[1])
    dq_ref[...] = jnp.where(lane < half, parts[0], parts[1]).astype(jnp.bfloat16)
    base = step * (2 * PAIR)
    cols = jnp.where(step == 0, jnp.zeros_like(cols_ref), cols_ref[...])
    for t, value in enumerate(lses + deltas):
        cols = jnp.where(lane == base + t, value, cols)
    cols_ref[...] = cols

    @pl.when(step == pl.num_programs(0) - 1)
    def _():
        rows_ref[...] = cols.T[: rows_ref.shape[0]]


def key_side_kernel(first, limits, k_ref, v_ref, *refs):
    groups, stats = refs[:3], refs[3:6]
    dk_ref, dv_ref, qcat, docat = refs[-4:]
    step = pl.program_id(0)
    rows, width = dk_ref.shape
    half = width // PAIR
    scale = half**-0.5
    base = (first + step) * (2 * PAIR)
    lane = lax.broadcasted_iota(jnp.int32, (rows, width), 1)
    live = lax.broadcasted_iota(jnp.int32, (rows, width), 0) < limits[NEAR]
    for k in range(NEAR):
        q = (groups[k // 3][k % 3, 0].astype(jnp.float32) * scale).astype(jnp.bfloat16)
        do = groups[k // 3][k % 3, 1]
        zero = jnp.zeros_like(q)
        for h in range(PAIR):
            mine = (lane < half) if h == 0 else (lane >= half)
            qcat[h, pl.ds(k * CELL, CELL), :] = jnp.where(mine, q, zero)
            docat[h, pl.ds(k * CELL, CELL), :] = jnp.where(mine, do, zero)
    own_keys = k_ref[...]
    own_values = v_ref[...]
    dk = dv = None
    for h in range(PAIR):
        lse = jnp.concatenate(
            [
                stats[k // 3][k % 3, pl.ds(base + h, 1), :]
                + jnp.where(limits[k] > 0, 0.0, 1e30)
                for k in range(NEAR)
            ],
            axis=1,
        )
        delta = jnp.concatenate(
            [stats[k // 3][k % 3, pl.ds(base + PAIR + h, 1), :] for k in range(NEAR)], axis=1
        )
        s = dot(own_keys, qcat[h], NT)
        p = jnp.exp(s - lse)
        dp = dot(own_values, docat[h], NT)
        ds = (p * (dp - delta)).astype(jnp.bfloat16)
        a = dot(p.astype(jnp.bfloat16), docat[h], NN)
        b = dot(ds, qcat[h], NN)
        dv = a if dv is None else dv + a
        dk = b if dk is None else dk + b
    dk_ref[...] = jnp.where(live, dk, 0.0).astype(jnp.bfloat16)
    dv_ref[...] = jnp.where(live, dv, 0.0).astype(jnp.bfloat16)


def near_specs(rows, width, pairs, near):
    specs, arrays = [], []
    for offset in (0, pairs):
        for array, slot in near:
            if slot is None:
                spec = pl.BlockSpec((rows, width), lambda i, *_, o=offset: (0, i + o))
            else:
                spec = pl.BlockSpec(
                    (None, rows, width), lambda i, *_, o=offset, s=slot: (s, 0, i + o)
                )
            specs.append(spec)
            arrays.append(array)
    return specs, arrays


def cost(rows, width, dots):
    return pl.CostEstimate(
        flops=2 * dots * NEAR * rows * CELL * width,
        bytes_accessed=(4 + 2 * NEAR) * rows * width * 2,
        transcendentals=NEAR * rows * CELL * width // 64,
    )


def query_side(limits, q, do, near, chunk, filled):
    rows, model_width = q.shape
    pairs = HEADS // PAIR // CHUNKS
    width = model_width // (HEADS // PAIR)
    first = chunk * pairs
    column = pl.BlockSpec((rows, width), lambda i, *_: (0, i + first))
    specs, arrays = near_specs(rows, width, pairs, near)
    in_specs = [column, column] + specs
    args = [q, do] + arrays
    aliases = {}
    for o, array in enumerate(filled):
        in_specs.append(pl.BlockSpec(memory_space=pl.ANY))
        args.append(array)
        aliases[len(args)] = o
    stat_rows = pairs * 2 * PAIR
    flat = jax.ShapeDtypeStruct((rows, model_width), jnp.bfloat16)
    return pl.pallas_call(
        query_side_kernel,
        grid_spec=pltpu.PrefetchScalarGridSpec(
            num_scalar_prefetch=1,
            grid=(pairs,),
            in_specs=in_specs,
            out_specs=[
                column,
                column,
                pl.BlockSpec((stat_rows, rows), lambda i, *_: (chunk, 0)),
            ],
            scratch_shapes=[pltpu.VMEM((rows, CELL), jnp.float32)]
            + [pltpu.VMEM((NEAR * CELL, width), jnp.bfloat16)] * 2,
        ),
        out_shape=[flat, flat, jax.ShapeDtypeStruct((stat_rows * CHUNKS, rows), jnp.float32)],
        input_output_aliases=aliases,
        cost_estimate=cost(rows, model_width // CHUNKS, 4),
        name="query_side",
    )(limits, *args)


def key_side(limits, k, v, groups, stats, first, pairs, filled):
    rows, model_width = k.shape
    width = model_width // (HEADS // PAIR)
    column = pl.BlockSpec((rows, width), lambda i, *_: (0, i + first))
    group = pl.BlockSpec((3, 2, rows, width), lambda i, *_: (0, 0, 0, i + first))
    whole = pl.BlockSpec(stats[0].shape, lambda i, *_: (0, 0, 0))
    flat = jax.ShapeDtypeStruct((rows, model_width), jnp.bfloat16)
    args = [k, v, *groups, *stats]
    in_specs = [column, column] + [group] * 3 + [whole] * 3
    aliases = {}
    for o, array in enumerate(filled):
        in_specs.append(pl.BlockSpec(memory_space=pl.ANY))
        args.append(array)
        aliases[len(args)] = o
    return pl.pallas_call(
        functools.partial(key_side_kernel, first),
        grid_spec=pltpu.PrefetchScalarGridSpec(
            num_scalar_prefetch=1,
            grid=(pairs,),
            in_specs=in_specs,
            out_specs=[column, column],
            scratch_shapes=[pltpu.VMEM((PAIR, NEAR * CELL, width), jnp.bfloat16)] * 2,
        ),
        out_shape=[flat, flat],
        input_output_aliases=aliases,
        cost_estimate=cost(rows, pairs * width, 4),
        name="key_side",
    )(limits, *args)


def partial_kernel(where, *refs):
    count = (len(refs) - 2) // 2
    grads, atts = refs[:count], refs[count : 2 * count]
    give_ref, keep_ref = refs[2 * count :]
    pieces = give_ref.shape[0]
    rows = give_ref.shape[1]
    total = None
    for g, a in zip(grads, atts):
        part = dot(g[...], a[...], TN)
        total = part if total is None else total + part
    total = total.reshape(pieces, 2, rows, total.shape[1])
    upper = where[1] == 1
    give_ref[...] = jnp.where(upper, total[:, 0], total[:, 1]).astype(jnp.bfloat16)
    keep_ref[...] = jnp.where(upper, total[:, 1], total[:, 0])


def partial_products(where, grads, atts, layers, places):
    atoms, width = atts[0].shape
    slab = width // layers
    rows = width // places
    shape = (places // 2, rows, slab)
    full = pl.BlockSpec((atoms, width), lambda i, w: (0, 0))
    cut = pl.BlockSpec((atoms, slab), lambda i, w: (0, w[0]))
    out = pl.BlockSpec(shape, lambda i, w: (0, 0, 0))
    return pl.pallas_call(
        partial_kernel,
        grid_spec=pltpu.PrefetchScalarGridSpec(
            num_scalar_prefetch=1,
            grid=(1,),
            in_specs=[full] * len(grads) + [cut] * len(atts),
            out_specs=[out, out],
        ),
        out_shape=[
            jax.ShapeDtypeStruct(shape, jnp.bfloat16),
            jax.ShapeDtypeStruct(shape, jnp.float32),
        ],
        name="partial",
    )(where, *grads, *atts)


def combine_kernel(where, keep_ref, got_ref, own_ref, *give_refs):
    pieces = keep_ref.shape[0]
    total = [keep_ref[i] + got_ref[i].astype(jnp.float32) for i in range(pieces)]
    me = where[2]

    def piece(index):
        value = total[0]
        for i in range(1, pieces):
            value = jnp.where(index == i, total[i], value)
        return value

    own_ref[...] = piece(me)
    for k, ref in enumerate(give_refs):
        ref[...] = piece(me ^ (k + 1)).astype(jnp.bfloat16)


def combine(where, keep, got):
    pieces, rows, slab = keep.shape
    here = pl.BlockSpec(memory_space=pltpu.VMEM)
    return pl.pallas_call(
        combine_kernel,
        in_specs=[pl.BlockSpec(memory_space=pltpu.SMEM), here, here],
        out_specs=[here] * pieces,
        out_shape=[jax.ShapeDtypeStruct((rows, slab), jnp.float32)]
        + [jax.ShapeDtypeStruct((rows, slab), jnp.bfloat16)] * (pieces - 1),
        name="combine",
    )(where, keep, got)


def place_kernel(where, *refs):
    out_ref = refs[-1]
    held = refs[:-1]
    slab = held[0].shape[1]
    layer = where[0]
    values = [h[...] for h in held]
    for target in range(len(held)):
        value = values[0]
        for o in range(1, len(held)):
            value = jnp.where(layer == (target ^ o), values[o], value)
        out_ref[:, target * slab : (target + 1) * slab] = value


def placed(where, held):
    rows, slab = held[0].shape
    shape = (rows, slab * len(held))
    here = pl.BlockSpec(memory_space=pltpu.VMEM)
    return pl.pallas_call(
        place_kernel,
        in_specs=[pl.BlockSpec(memory_space=pltpu.SMEM)] + [here] * len(held),
        out_specs=here,
        out_shape=jax.ShapeDtypeStruct(shape, jnp.float32),
        name="placed",
    )(where, *held)


def even_pairs(count):
    pairs = [(i, i + 1) for i in range(0, count - 1, 2)]
    return pairs + [(b, a) for a, b in pairs]


def odd_pairs(count):
    pairs = [(i, i + 1) for i in range(1, count - 1, 2)]
    return pairs + [(b, a) for a, b in pairs]


def flip_pairs(count, by):
    return [(i, i ^ by) for i in range(count)]


def relay_ring(count):
    return [(i, (i + (2 if i % 2 == 0 else -2)) % count) for i in range(count)]


def in_partner_order(table, index, axis):
    low, own, high = (lax.index_in_dim(table, i, axis) for i in range(3))
    first = jnp.where(index % 2 == 0, high, low)
    second = jnp.where(index % 2 == 0, low, high)
    return jnp.concatenate([own, first, second], axis=axis)


def body(queries, keys, values, out_grad, out_weight, pair_counts, counts):
    row_count, model_width = queries.shape
    layers = lax.axis_size("dz")
    places = lax.axis_size("dxy")
    layer = lax.axis_index("dz")
    place = lax.axis_index("dxy")
    chunk_width = model_width // CHUNKS
    near_y = even_pairs(places)
    near_z = relay_ring(places)
    core = even_pairs(layers)
    mid = odd_pairs(layers)

    owns, near = [], []
    for c in range(CHUNKS):
        columns = slice(c * chunk_width, (c + 1) * chunk_width)
        owns.append(jnp.concatenate([keys[:, columns], values[:, columns]], axis=1))
    both = jnp.stack(owns)
    core_own = lax.ppermute(both, "dz", core)
    mid_own = lax.ppermute(both, "dz", mid)
    for c in range(CHUNKS):
        even = lax.ppermute(owns[c], "dxy", near_y)
        odd = lax.ppermute(even, "dxy", near_z)
        slots = [(owns[c], None), (even, None), (odd, None)]
        if c == 0:
            for pairs, own in ((core, core_own), (mid, mid_own)):
                slots.append((own, c))
                for value in (even, odd):
                    slots.append((lax.ppermute(value, "dz", pairs), None))
        else:
            both = jnp.stack([even, odd])
            for pairs, own in ((core, core_own), (mid, mid_own)):
                got = lax.ppermute(both, "dz", pairs)
                slots += [(own, c), (got, 0), (got, 1)]
        near.append(slots)

    atom_index = jnp.arange(CELL, dtype=jnp.int32)
    table = pair_counts.reshape(3, 3)
    near_limits = in_partner_order(in_partner_order(table, layer, 0), place, 1).reshape(NEAR)
    limits = jnp.concatenate([near_limits, counts])
    where = jnp.stack([layer, place % 2, place // 2]).astype(jnp.int32)
    live_rows = (atom_index[None, :] < counts[:, None]).reshape(row_count, 1)
    masked_grad = jnp.where(live_rows, out_grad, jnp.zeros_like(out_grad))
    out_delta = jnp.dot(masked_grad, out_weight, preferred_element_type=jnp.float32).astype(
        jnp.bfloat16
    )

    own = jnp.stack([queries, out_delta])
    even = lax.ppermute(own, "dxy", near_y)
    odd = lax.ppermute(even, "dxy", near_z)
    columns = jnp.stack([own, even, odd])
    groups = [columns, lax.ppermute(columns, "dz", core), lax.ppermute(columns, "dz", mid)]

    grads = [masked_grad]
    for bit in [1 << b for b in reversed(range(bits_of(layers)))]:
        grads = grads + [lax.ppermute(g, "dz", flip_pairs(layers, bit)) for g in grads]

    filled = []
    for c in range(CHUNKS):
        filled = query_side(limits, queries, out_delta, near[c], c, filled)
    att, dq, own = filled

    even = lax.ppermute(own, "dxy", near_y)
    odd = lax.ppermute(even, "dxy", near_z)
    columns = jnp.stack([own, even, odd])
    stats = [columns, lax.ppermute(columns, "dz", core), lax.ppermute(columns, "dz", mid)]

    atts = [att]
    for bit in [1 << b for b in reversed(range(bits_of(layers)))]:
        atts = atts + [lax.ppermute(a, "dz", flip_pairs(layers, bit)) for a in atts]
    give, keep = partial_products(where, grads, atts, layers, places)
    got = lax.ppermute(give, "dxy", flip_pairs(places, 1))
    bit = 2
    while places // bit > 4:
        upper = (place // bit) % 2
        halves = (keep + got.astype(jnp.float32)).reshape((places // bit // 2, 2) + keep.shape[1:])
        give = lax.dynamic_index_in_dim(halves, 1 - upper, 1, keepdims=False)
        keep = lax.dynamic_index_in_dim(halves, upper, 1, keepdims=False)
        got = lax.ppermute(give.astype(jnp.bfloat16), "dxy", flip_pairs(places, bit))
        bit *= 2
    where = where.at[2].set(place // bit)
    own, *gives = combine(where, keep, got)
    gots = [
        lax.ppermute(give, "dxy", flip_pairs(places, bit * (k + 1)))
        for k, give in enumerate(gives)
    ]
    for got in gots:
        own = own + got.astype(jnp.float32)
    held = [own * ((row_count * layers * places) ** -0.5)]
    order = [0]
    for bit in [1 << b for b in reversed(range(bits_of(layers)))]:
        held = held + [lax.ppermute(h, "dz", flip_pairs(layers, bit)) for h in held]
        order = order + [o ^ bit for o in order]
    wo_grad = placed(where, [held[order.index(o)] for o in range(layers)])

    filled = []
    first = 0
    for pairs in KEY_PARTS:
        filled = key_side(limits, keys, values, groups, stats, first, pairs, filled)
        first += pairs
    dk, dv = filled
    return dq, dk, dv, wo_grad


def solution(mesh):
    in_specs = (
        P(("dz", "dxy"), None),
        P(("dz", "dxy"), None),
        P(("dz", "dxy"), None),
        P(("dz", "dxy"), None),
        P(),
        P(("dz", "dxy"), None),
        P(("dz", "dxy")),
    )
    out_specs = (
        P(("dz", "dxy"), None),
        P(("dz", "dxy"), None),
        P(("dz", "dxy"), None),
        P("dxy", None),
    )
    return jax.shard_map(body, mesh=mesh, in_specs=in_specs, out_specs=out_specs, check_vma=False)
```

```python
import functools

import jax
import jax.numpy as jnp
from jax import lax
from jax.experimental import pallas as pl
from jax.experimental.pallas import tpu as pltpu
from jax.sharding import PartitionSpec as P

HEADS = 16
CELL = 128
PAIR = 2
NEAR = 9
CHUNKS = 2
KEY_PARTS = 2
ALIGN = 16
LEVELS = (512, 640, 896, 1152)
UNROLL = 2


NT = (((1,), (1,)), ((), ()))
NN = (((1,), (0,)), ((), ()))
TN = (((0,), (0,)), ((), ()))


def dot(a, b, dims):
    return lax.dot_general(a, b, dims, preferred_element_type=jnp.float32)


GRANT = pltpu.CompilerParams(vmem_limit_bytes=16 * 1024 * 1024)


def bits_of(count):
    return count.bit_length() - 1


def packed_offsets(limits):
    offsets = [jnp.int32(0)]
    for k in range(NEAR):
        offsets.append(offsets[-1] + (limits[k] + (ALIGN - 1)) // ALIGN * ALIGN)
    return [pl.multiple_of(o, ALIGN) for o in offsets[:-1]], offsets[-1]


def by_level(total, body):
    low = 0
    for level in LEVELS:
        pl.when((total > low) & (total <= level))(lambda n=level: body(n))
        low = level


def stacked_heads(block, lane):
    zero = jnp.zeros_like(block)
    half = block.shape[1] // PAIR
    return jnp.concatenate(
        [jnp.where(lane < half, block, zero), jnp.where(lane >= half, block, zero)], axis=0
    )


def query_side_kernel(slots, count, limits, q_ref, do_ref, *refs):
    att_ref, dq_ref, rows_ref, cols_ref, bias_ref, kcat, vcat = refs[-7:]
    group = pl.program_id(0)
    rows, width = q_ref.shape[0], q_ref.shape[1] // UNROLL
    half = width // PAIR
    scale = half**-0.5
    lane = lax.broadcasted_iota(jnp.int32, (rows, width), 1)
    offsets, total = packed_offsets(limits)

    @pl.when(group == 0)
    def _():
        kcat[...] = jnp.zeros_like(kcat)
        vcat[...] = jnp.zeros_like(vcat)
        at = lax.broadcasted_iota(jnp.int32, bias_ref.shape, 1)
        bias = jnp.full(bias_ref.shape, -1e30, jnp.float32)
        for k in range(NEAR):
            inside = (at >= offsets[k]) & (at < offsets[k] + limits[k])
            bias = jnp.where(inside, 0.0, bias)
        bias_ref[...] = bias
        cols_ref[...] = jnp.zeros_like(cols_ref)

    def near_block(k, shift, columns):
        index, slot = slots[k]
        ref = refs[index + shift * count]
        return ref[:, columns] if slot is None else ref[slot, :, columns]

    def pair(n, u):
        columns = slice(u * width, (u + 1) * width)
        for k in range(NEAR):
            kcat[u, pl.ds(offsets[k], CELL), :] = near_block(k, 0, columns)
            vcat[u, pl.ds(offsets[k], CELL), :] = near_block(k, 1, columns)
        keys, values = kcat[u, :n], vcat[u, :n]
        q = q_ref[:, columns]
        q = stacked_heads((q.astype(jnp.float32) * scale).astype(jnp.bfloat16), lane)
        do = stacked_heads(do_ref[:, columns], lane)
        s = dot(q, keys, NT) + bias_ref[:, :n]
        top = jnp.max(s, axis=1, keepdims=True)
        p = jnp.exp(s - top)
        weight = jnp.sum(p, axis=1, keepdims=True)
        inverse = 1.0 / weight
        out = (dot(p.astype(jnp.bfloat16), values, NN) * inverse).astype(jnp.bfloat16)
        product = do.astype(jnp.float32) * out.astype(jnp.float32)
        delta = jnp.sum(product, axis=1, keepdims=True)
        ds = (p * (dot(do, values, NT) - delta)).astype(jnp.bfloat16)
        dq = dot(ds, keys, NN) * (inverse * scale)
        att_ref[:, columns] = jnp.where(lane < half, out[:rows], out[rows:])
        dq = jnp.where(lane < half, dq[:rows], dq[rows:])
        dq_ref[:, columns] = dq.astype(jnp.bfloat16)
        lse = top + jnp.log(weight)
        return lse[:rows], lse[rows:], delta[:rows], delta[rows:]

    def body(n):
        values = []
        for u in range(UNROLL):
            values += pair(n, u)
        cols = cols_ref[...]
        for t, value in enumerate(values):
            cols = jnp.where(lane == group * (2 * PAIR * UNROLL) + t, value, cols)
        cols_ref[...] = cols

    by_level(total, body)

    @pl.when(group == pl.num_programs(0) - 1)
    def _():
        rows_ref[...] = cols_ref[...].T[: rows_ref.shape[0]]


def key_side_kernel(first, limits, k_ref, v_ref, *refs):
    groups, stats = refs[:3], refs[3:6]
    dk_ref, dv_ref, stat_ref, spare_ref, qcat, docat = refs[-6:]
    group = pl.program_id(0)
    rows, width = dk_ref.shape[0], dk_ref.shape[1] // UNROLL
    half = width // PAIR
    scale = half**-0.5
    lane = lax.broadcasted_iota(jnp.int32, (rows, width), 1)
    live = lax.broadcasted_iota(jnp.int32, (rows, width), 0) < limits[NEAR]
    offsets, total = packed_offsets(limits)
    stat_rows = stats[0].shape[1]

    @pl.when(group == 0)
    def _():
        qcat[...] = jnp.zeros_like(qcat)
        docat[...] = jnp.zeros_like(docat)
        spare_ref[...] = jnp.zeros_like(spare_ref)
        kind = lax.broadcasted_iota(jnp.int32, (stat_rows, CELL), 0) % (2 * PAIR)
        rest = jnp.zeros((CELL - stat_rows, CELL), jnp.float32)
        for k in range(NEAR):
            value = stats[k // 3][k % 3]
            linked = jnp.where(limits[k] > 0, 0.0, 1e30)
            value = jnp.where(kind < PAIR, value + linked, value)
            spare_ref[pl.ds(offsets[k], CELL), :] = jnp.concatenate([value, rest], axis=0).T
        for k in range(NEAR):
            piece = spare_ref[k * CELL : (k + 1) * CELL, :].T
            stat_ref[:, k * CELL : (k + 1) * CELL] = piece[:stat_rows]

    def pair(n, u):
        columns = slice(u * width, (u + 1) * width)
        base = (first + group * UNROLL + u) * (2 * PAIR)
        for h in range(PAIR):
            mine = (lane < half) if h == 0 else (lane >= half)
            for k in range(NEAR):
                at = pl.ds(pl.multiple_of(offsets[k] + h * n, ALIGN), CELL)
                q = groups[k // 3][k % 3, 0, :, columns]
                q = (q.astype(jnp.float32) * scale).astype(jnp.bfloat16)
                do = groups[k // 3][k % 3, 1, :, columns]
                qcat[u, at, :] = jnp.where(mine, q, jnp.zeros_like(q))
                docat[u, at, :] = jnp.where(mine, do, jnp.zeros_like(do))
        lse, delta = (
            jnp.concatenate(
                [stat_ref[pl.ds(base + o + h, 1), :n] for h in range(PAIR)], axis=1
            )
            for o in (0, PAIR)
        )
        qs, dos = qcat[u, : PAIR * n], docat[u, : PAIR * n]
        p = jnp.exp(dot(k_ref[:, columns], qs, NT) - lse)
        dp = dot(v_ref[:, columns], dos, NT)
        ds = (p * (dp - delta)).astype(jnp.bfloat16)
        dv = dot(p.astype(jnp.bfloat16), dos, NN)
        dk = dot(ds, qs, NN)
        dk_ref[:, columns] = jnp.where(live, dk, 0.0).astype(jnp.bfloat16)
        dv_ref[:, columns] = jnp.where(live, dv, 0.0).astype(jnp.bfloat16)

    def body(n):
        for u in range(UNROLL):
            pair(n, u)

    by_level(total, body)


def cost(rows, width, dots):
    return pl.CostEstimate(
        flops=2 * dots * NEAR * rows * CELL * width,
        bytes_accessed=(4 + 2 * NEAR) * rows * width * 2,
        transcendentals=NEAR * rows * CELL * width // 64,
    )


def query_side(limits, q, do, arrays, slots, chunk, filled):
    rows, model_width = q.shape
    width = model_width // (HEADS // PAIR)
    stat_rows = HEADS * 2
    wide = width * UNROLL
    groups = model_width // CHUNKS // wide
    column = pl.BlockSpec((rows, wide), lambda i, *_: (0, chunk * groups + i))
    in_specs = [column, column]
    for shift in (0, groups):
        for array, part in arrays:
            if array.ndim == 2:
                spec = pl.BlockSpec((rows, wide), lambda i, *_, s=shift: (0, s + i))
            else:
                lead = array.shape[0] if part is None else None
                spec = pl.BlockSpec(
                    (lead, rows, wide), lambda i, *_, s=shift, p=part or 0: (p, 0, s + i)
                )
            in_specs.append(spec)
    in_specs += [pl.BlockSpec(memory_space=pl.ANY)] * len(filled)
    args = [q, do] + [array for array, _ in arrays] * 2 + list(filled)
    aliases = {len(args) - len(filled) + 1 + o: o for o in range(len(filled))}
    flat = jax.ShapeDtypeStruct((rows, model_width), jnp.bfloat16)
    return pl.pallas_call(
        functools.partial(query_side_kernel, slots, len(arrays)),
        grid_spec=pltpu.PrefetchScalarGridSpec(
            num_scalar_prefetch=1,
            grid=(groups,),
            in_specs=in_specs,
            out_specs=[
                column,
                column,
                pl.BlockSpec((stat_rows // CHUNKS, rows), lambda i, *_: (chunk, 0)),
            ],
            scratch_shapes=[
                pltpu.VMEM((rows, CELL), jnp.float32),
                pltpu.VMEM((1, NEAR * CELL), jnp.float32),
            ]
            + [pltpu.VMEM((UNROLL, NEAR * CELL, width), jnp.bfloat16)] * 2,
        ),
        out_shape=[flat, flat, jax.ShapeDtypeStruct((stat_rows, rows), jnp.float32)],
        input_output_aliases=aliases,
        cost_estimate=cost(rows, model_width // CHUNKS, 4),
        compiler_params=GRANT,
        name="query_side",
    )(limits, *args)


def key_side(limits, k, v, groups, stats, part, filled):
    rows, model_width = k.shape
    parts = KEY_PARTS
    pairs = HEADS // PAIR // parts
    width = model_width // (HEADS // PAIR)
    wide = width * UNROLL
    steps = pairs // UNROLL
    column = pl.BlockSpec((rows, wide), lambda i, *_: (0, part * steps + i))
    group = pl.BlockSpec((3, 2, rows, wide), lambda i, *_: (0, 0, 0, part * steps + i))
    whole = pl.BlockSpec(stats[0].shape, lambda i, *_: (0, 0, 0))
    flat = jax.ShapeDtypeStruct((rows, model_width), jnp.bfloat16)
    args = [k, v, *groups, *stats, *filled]
    aliases = {len(args) - len(filled) + 1 + o: o for o in range(len(filled))}
    return pl.pallas_call(
        functools.partial(key_side_kernel, part * pairs),
        grid_spec=pltpu.PrefetchScalarGridSpec(
            num_scalar_prefetch=1,
            grid=(steps,),
            in_specs=[column] * 2
            + [group] * 3
            + [whole] * 3
            + [pl.BlockSpec(memory_space=pl.ANY)] * len(filled),
            out_specs=[column] * 2,
            scratch_shapes=[
                pltpu.VMEM((stats[0].shape[1], NEAR * CELL), jnp.float32),
                pltpu.VMEM((NEAR * CELL, CELL), jnp.float32),
            ]
            + [pltpu.VMEM((UNROLL, (PAIR * NEAR + 1) * CELL, width), jnp.bfloat16)] * 2,
        ),
        out_shape=[flat, flat],
        input_output_aliases=aliases,
        cost_estimate=cost(rows, pairs * width, 4),
        compiler_params=GRANT,
        name="key_side",
    )(limits, *args)


def join_kernel(*refs):
    out_ref = refs[-1]
    for k in range(6):
        out_ref[k // 2, k % 2] = refs[k][...]


def joined(*columns):
    rows, model_width = columns[0][0].shape
    wide = model_width // 2
    block = pl.BlockSpec((rows, wide), lambda i: (0, i))
    return pl.pallas_call(
        join_kernel,
        grid=(2,),
        in_specs=[block] * 6,
        out_specs=pl.BlockSpec((3, 2, rows, wide), lambda i: (0, 0, 0, i)),
        out_shape=jax.ShapeDtypeStruct((3, 2, rows, model_width), jnp.bfloat16),
        compiler_params=GRANT,
        name="join",
    )(*columns[0], *columns[1], *columns[2])


def partial_kernel(where, *refs):
    count = (len(refs) - 2) // 2
    grads, atts = refs[:count], refs[count : 2 * count]
    give_ref, keep_ref = refs[2 * count :]
    pieces = give_ref.shape[0]
    rows = give_ref.shape[1]
    total = None
    for g, a in zip(grads, atts):
        part = dot(g[...], a[...], TN)
        total = part if total is None else total + part
    total = total.reshape(pieces, 2, rows, total.shape[1])
    upper = where[1] == 1
    give_ref[...] = jnp.where(upper, total[:, 0], total[:, 1]).astype(jnp.bfloat16)
    keep_ref[...] = jnp.where(upper, total[:, 1], total[:, 0])


def partial_products(where, grads, atts, layers, places):
    atoms, width = atts[0].shape
    slab = width // layers
    rows = width // places
    shape = (places // 2, rows, slab)
    full = pl.BlockSpec((atoms, width), lambda i, w: (0, 0))
    cut = pl.BlockSpec((atoms, slab), lambda i, w: (0, w[0]))
    out = pl.BlockSpec(shape, lambda i, w: (0, 0, 0))
    return pl.pallas_call(
        partial_kernel,
        grid_spec=pltpu.PrefetchScalarGridSpec(
            num_scalar_prefetch=1,
            grid=(1,),
            in_specs=[full] * len(grads) + [cut] * len(atts),
            out_specs=[out, out],
        ),
        out_shape=[
            jax.ShapeDtypeStruct(shape, jnp.bfloat16),
            jax.ShapeDtypeStruct(shape, jnp.float32),
        ],
        compiler_params=GRANT,
        name="partial",
    )(where, *grads, *atts)


def combine_kernel(where, keep_ref, got_ref, own_ref, *give_refs):
    pieces = keep_ref.shape[0]
    total = [keep_ref[i] + got_ref[i].astype(jnp.float32) for i in range(pieces)]
    me = where[2]

    def piece(index):
        value = total[0]
        for i in range(1, pieces):
            value = jnp.where(index == i, total[i], value)
        return value

    own_ref[...] = piece(me)
    for k, ref in enumerate(give_refs):
        ref[...] = piece(me ^ (k + 1)).astype(jnp.bfloat16)


def combine(where, keep, got):
    pieces, rows, slab = keep.shape
    here = pl.BlockSpec(memory_space=pltpu.VMEM)
    return pl.pallas_call(
        combine_kernel,
        in_specs=[pl.BlockSpec(memory_space=pltpu.SMEM), here, here],
        out_specs=[here] * pieces,
        out_shape=[jax.ShapeDtypeStruct((rows, slab), jnp.float32)]
        + [jax.ShapeDtypeStruct((rows, slab), jnp.bfloat16)] * (pieces - 1),
        compiler_params=GRANT,
        name="combine",
    )(where, keep, got)


def place_kernel(where, *refs):
    out_ref = refs[-1]
    held = refs[:-1]
    slab = held[0].shape[1]
    layer = where[0]
    values = [h[...] for h in held]
    for target in range(len(held)):
        value = values[0]
        for o in range(1, len(held)):
            value = jnp.where(layer == (target ^ o), values[o], value)
        out_ref[:, target * slab : (target + 1) * slab] = value


def placed(where, held):
    rows, slab = held[0].shape
    shape = (rows, slab * len(held))
    here = pl.BlockSpec(memory_space=pltpu.VMEM)
    return pl.pallas_call(
        place_kernel,
        in_specs=[pl.BlockSpec(memory_space=pltpu.SMEM)] + [here] * len(held),
        out_specs=here,
        out_shape=jax.ShapeDtypeStruct(shape, jnp.float32),
        compiler_params=GRANT,
        name="placed",
    )(where, *held)


def even_pairs(count):
    pairs = [(i, i + 1) for i in range(0, count - 1, 2)]
    return pairs + [(b, a) for a, b in pairs]


def odd_pairs(count):
    pairs = [(i, i + 1) for i in range(1, count - 1, 2)]
    return pairs + [(b, a) for a, b in pairs]


def flip_pairs(count, by):
    return [(i, i ^ by) for i in range(count)]


def relay_ring(count):
    return [(i, (i + (2 if i % 2 == 0 else -2)) % count) for i in range(count)]


def in_partner_order(table, index, axis):
    low, own, high = (lax.index_in_dim(table, i, axis) for i in range(3))
    first = jnp.where(index % 2 == 0, high, low)
    second = jnp.where(index % 2 == 0, low, high)
    return jnp.concatenate([own, first, second], axis=axis)


def body(queries, keys, values, out_grad, out_weight, pair_counts, counts):
    row_count, model_width = queries.shape
    layers = lax.axis_size("dz")
    places = lax.axis_size("dxy")
    layer = lax.axis_index("dz")
    place = lax.axis_index("dxy")
    chunk_width = model_width // CHUNKS
    near_y = even_pairs(places)
    near_z = relay_ring(places)
    core = even_pairs(layers)
    mid = odd_pairs(layers)

    owns, near = [], []
    for c in range(CHUNKS):
        columns = slice(c * chunk_width, (c + 1) * chunk_width)
        owns.append(jnp.concatenate([keys[:, columns], values[:, columns]], axis=1))
    both = jnp.stack(owns)
    core_own = lax.ppermute(both, "dz", core)
    mid_own = lax.ppermute(both, "dz", mid)
    for c in range(CHUNKS):
        even = lax.ppermute(owns[c], "dxy", near_y)
        odd = lax.ppermute(even, "dxy", near_z)
        both = jnp.stack([even, odd])
        arrays = [(owns[c], None), (both, None), (core_own, c), (mid_own, c)]
        for pairs in (core, mid):
            arrays.append((lax.ppermute(both, "dz", pairs), None))
        near.append(arrays)
    slots = []
    for own, both in ((0, 1), (2, 4), (3, 5)):
        slots += [(own, None), (both, 0), (both, 1)]

    atom_index = jnp.arange(CELL, dtype=jnp.int32)
    table = pair_counts.reshape(3, 3)
    near_limits = in_partner_order(in_partner_order(table, layer, 0), place, 1).reshape(NEAR)
    limits = jnp.concatenate([near_limits, counts])
    where = jnp.stack([layer, place % 2, place // 2]).astype(jnp.int32)
    live_rows = (atom_index[None, :] < counts[:, None]).reshape(row_count, 1)
    masked_grad = jnp.where(live_rows, out_grad, jnp.zeros_like(out_grad))
    out_delta = jnp.dot(masked_grad, out_weight, preferred_element_type=jnp.float32).astype(
        jnp.bfloat16
    )

    spread = []
    for own in (queries, out_delta):
        even = lax.ppermute(own, "dxy", near_y)
        odd = lax.ppermute(even, "dxy", near_z)
        spread.append((own, even, odd))
    columns = joined(*zip(*spread))
    groups = [
        columns, lax.ppermute(columns, "dz", core), lax.ppermute(columns, "dz", mid)
    ]

    grads = [masked_grad]
    for bit in [1 << b for b in reversed(range(bits_of(layers)))]:
        grads = grads + [lax.ppermute(g, "dz", flip_pairs(layers, bit)) for g in grads]

    filled = []
    for c in range(CHUNKS):
        filled = query_side(limits, queries, out_delta, near[c], slots, c, filled)
    att, dq, own = filled

    even = lax.ppermute(own, "dxy", near_y)
    odd = lax.ppermute(even, "dxy", near_z)
    columns = jnp.stack([own, even, odd])
    stats = [
        columns, lax.ppermute(columns, "dz", core), lax.ppermute(columns, "dz", mid)
    ]

    atts = [att]
    for bit in [1 << b for b in reversed(range(bits_of(layers)))]:
        atts = atts + [lax.ppermute(a, "dz", flip_pairs(layers, bit)) for a in atts]
    give, keep = partial_products(where, grads, atts, layers, places)
    got = lax.ppermute(give, "dxy", flip_pairs(places, 1))
    bit = 2
    while places // bit > 4:
        upper = (place // bit) % 2
        halves = (keep + got.astype(jnp.float32)).reshape((places // bit // 2, 2) + keep.shape[1:])
        give = lax.dynamic_index_in_dim(halves, 1 - upper, 1, keepdims=False)
        keep = lax.dynamic_index_in_dim(halves, upper, 1, keepdims=False)
        got = lax.ppermute(give.astype(jnp.bfloat16), "dxy", flip_pairs(places, bit))
        bit *= 2
    where = where.at[2].set(place // bit)
    own, *gives = combine(where, keep, got)
    gots = [
        lax.ppermute(give, "dxy", flip_pairs(places, bit * (k + 1)))
        for k, give in enumerate(gives)
    ]
    for got in gots:
        own = own + got.astype(jnp.float32)
    held = [own * ((row_count * layers * places) ** -0.5)]
    order = [0]
    for bit in [1 << b for b in reversed(range(bits_of(layers)))]:
        held = held + [lax.ppermute(h, "dz", flip_pairs(layers, bit)) for h in held]
        order = order + [o ^ bit for o in order]
    wo_grad = placed(where, [held[order.index(o)] for o in range(layers)])

    filled = []
    for part in range(KEY_PARTS):
        filled = key_side(limits, keys, values, groups, stats, part, filled)
    dk, dv = filled
    return dq, dk, dv, wo_grad


def solution(mesh):
    in_specs = (
        P(("dz", "dxy"), None),
        P(("dz", "dxy"), None),
        P(("dz", "dxy"), None),
        P(("dz", "dxy"), None),
        P(),
        P(("dz", "dxy"), None),
        P(("dz", "dxy")),
    )
    out_specs = (
        P(("dz", "dxy"), None),
        P(("dz", "dxy"), None),
        P(("dz", "dxy"), None),
        P("dxy", None),
    )
    return jax.shard_map(body, mesh=mesh, in_specs=in_specs, out_specs=out_specs, check_vma=False)
```
